32 devices in a mesh: rep: 8 (over z, x), mp: 4 (over y, core).
Axes of the slice: x: 2, y: 2, z: 4, core: 2. Of those that a mesh axis runs over, the one named last changes fastest.
Arguments:
- weight: bfloat16 [4096, 4096], P('rep', 'mp'), may hold values from -4 to 4
- tokens: bfloat16 [2048, 4096], P('rep', 'mp'), may hold values from -16 to 16
- cotangent: bfloat16 [2048, 4096], P('rep', 'mp'), may hold values from -128 to 128
- next_tokens: bfloat16 [2048, 4096], P('rep'), may hold values from -6 to 6
Outputs:
- new_weight: bfloat16 [4096, 4096], P('rep', 'mp')
- next_query: bfloat16 [2048, 4096], P('rep', 'mp')
The draws below stay inside these ranges and needn't reach their ends.
All inputs are finite; a program needn't handle non-finite values.
Results may differ from the reference program's by a relative error of at most 0.0049.
Values may be sent and summed in bfloat16 or wider, within the bound.
A program may use at most 128 MiB of HBM per device.

```python
import jax
import jax.numpy as jnp

D = 4096
TOK_DEV = 256
GRADIENT_TOKENS = 2048
NEXT = 2048


def shared_weights(key, copies):
    freqs = jax.random.uniform(jax.random.fold_in(key, 1), (copies, 1), minval=0.5, maxval=2.5)
    phases = jax.random.uniform(jax.random.fold_in(key, 2), (copies, 1), minval=0.0, maxval=6.2831853)
    position = (jnp.arange(D).astype(jnp.float32) / D)[None, :]
    waves = jnp.cos(6.2831853 * freqs * position + phases)
    return jnp.repeat(waves, TOK_DEV, axis=0)


def row_weights(key):
    position = jnp.arange(GRADIENT_TOKENS) % TOK_DEV
    base = jnp.where(position < TOK_DEV // 4, 0.3, 1.2).astype(jnp.float32)
    spike_amount = jax.random.bernoulli(jax.random.fold_in(key, 99), 0.03, (GRADIENT_TOKENS,))
    amplify_factor = jnp.where(spike_amount, 3.0, 1.0).astype(jnp.float32)
    return (base * amplify_factor)[:, None]


def draw_tokens(key, part):
    copies = GRADIENT_TOKENS // TOK_DEV
    mixing = shared_weights(jax.random.fold_in(key, 17), copies)
    mixing_strength = row_weights(key)
    shared = jnp.clip(jax.random.normal(jax.random.fold_in(key, 11), (TOK_DEV, D)), -4.0, 4.0)
    owned = jnp.clip(jax.random.normal(jax.random.fold_in(key, 12), (GRADIENT_TOKENS, D)), -4.0, 4.0)
    values = mixing_strength * mixing * jnp.tile(shared, (copies, 1)) + 0.5 * owned
    return jnp.clip(values, -16.0, 16.0).astype(jnp.bfloat16)


def draw_cotangent(key, part):
    copies = GRADIENT_TOKENS // TOK_DEV
    mixing = shared_weights(jax.random.fold_in(key, 27), copies)
    mixing_strength = row_weights(key)
    owner_replica = (jnp.arange(GRADIENT_TOKENS) // TOK_DEV).astype(jnp.float32)
    replica_scale = (1.0 + 2.0 * owner_replica / max(copies - 1, 1))[:, None]
    heavy = jax.random.bernoulli(jax.random.fold_in(key, 31), 0.01, (1, D))
    shared = jnp.clip(jax.random.normal(jax.random.fold_in(key, 21), (TOK_DEV, D)), -4.0, 4.0)
    owned = jnp.clip(jax.random.normal(jax.random.fold_in(key, 22), (GRADIENT_TOKENS, D)), -4.0, 4.0)
    drawn_scale = (1.0 + 2.0 * jnp.arange(D).astype(jnp.float32) / (D - 1))[None, :]
    column_scale = jnp.where(heavy, 15.0, drawn_scale)
    values = (mixing_strength * mixing * jnp.tile(shared, (copies, 1)) + 0.5 * owned) * replica_scale * column_scale
    return jnp.clip(values, -128.0, 128.0).astype(jnp.bfloat16)


def levels(key, shape, shards, least, top_value):
    level = 1.0
    for axis_at, blocks in shards:
        draws = jax.random.uniform(jax.random.fold_in(jax.random.fold_in(key, 6), axis_at), (blocks,), jnp.float32, least / len(shards), top_value / len(shards))
        level = level * jnp.repeat(jnp.exp(draws), shape[axis_at] // blocks).reshape((-1,) + (1,) * (len(shape) - 1 - axis_at))
    return level


def gaussian(stream_key, dims, deviation, limit, shards=(), held_as=jnp.bfloat16):
    loudness = levels(stream_key, dims, shards, -0.22, 0.18) if shards else 1.0
    result = jax.random.normal(stream_key, dims, jnp.float32) * deviation * loudness
    return jnp.minimum(jnp.maximum(result, -limit), limit).astype(held_as)


def setup_inputs(seed: int = 0) -> dict:
    keys = jax.random.split(jax.random.key(seed), 5)
    weight = gaussian(keys[0], (D, D), 1.0, 4.0, ((0, 8), (1, 4)))
    tokens = draw_tokens(jax.random.fold_in(keys[4], 71), 0)
    cotangent = draw_cotangent(jax.random.fold_in(keys[4], 71), 0)
    next_tokens = gaussian(keys[3], (NEXT, D), 1.0, 6.0, ((0, 8),))
    return dict(weight=weight, tokens=tokens, cotangent=cotangent, next_tokens=next_tokens)


learning_rate = 0.002
eps = 1e-06

def combine(first, second):
    cross_dot = jnp.sum(first * second)
    first_sq = jnp.sum(first * first)
    second_sq = jnp.sum(second * second)
    return (1.0 - cross_dot / (2.0 * first_sq + eps)) * first + (1.0 - cross_dot / (2.0 * second_sq + eps)) * second

def reference(weight, tokens, cotangent, next_tokens):
    replicas = GRADIENT_TOKENS // TOK_DEV

    def leaf_grad(index):
        token_rows = tokens[index * TOK_DEV:(index + 1) * TOK_DEV]
        grad_rows = cotangent[index * TOK_DEV:(index + 1) * TOK_DEV]
        return jnp.dot(token_rows.T, grad_rows, preferred_element_type=jnp.float32)

    def node(index, stride):
        if stride == replicas:
            return leaf_grad(index)
        return combine(node(index, 2 * stride), node(index + stride, 2 * stride))
    update = node(0, 1)
    new_weight = (weight.astype(jnp.float32) - learning_rate * update).astype(jnp.bfloat16)
    product = jnp.dot(next_tokens, new_weight, preferred_element_type=jnp.float32)
    next_query = (product * D ** (-0.5)).astype(jnp.bfloat16)
    return (new_weight, next_query)
```

```python
import jax
import jax.numpy as jnp
from jax import lax
from jax.sharding import PartitionSpec as P

learning_rate = 0.002
eps = 1e-06
HI = lax.Precision.HIGHEST


def mix(gram, replicas):
    mixing = jnp.eye(replicas, dtype=jnp.float32)
    count = replicas
    while count > 1:
        middle = count // 2
        lower = mixing[:middle]
        upper = mixing[middle:count]
        lower_gram = jnp.dot(lower, gram, precision=HI)
        upper_gram = jnp.dot(upper, gram, precision=HI)
        cross = jnp.sum(lower_gram * upper, axis=1)
        lower_sq = jnp.sum(lower_gram * lower, axis=1)
        upper_sq = jnp.sum(upper_gram * upper, axis=1)
        mixing = (1.0 - cross / (2.0 * lower_sq + eps))[:, None] * lower + (
            1.0 - cross / (2.0 * upper_sq + eps)
        )[:, None] * upper
        count = middle
    return mixing[0]


def local(weight, tokens, cotangent, next_tokens):
    replicas = lax.axis_size("rep")
    per, width = cotangent.shape
    rows = weight.shape[0]
    cots = lax.all_gather(cotangent, "rep", axis=0, tiled=False)
    own = lax.all_gather(tokens, "mp", axis=1, tiled=True)
    stacked = own.reshape(per, replicas, rows).transpose(1, 0, 2)
    toks = lax.all_to_all(stacked, "rep", split_axis=0, concat_axis=0, tiled=True)
    grads = [
        lax.dot_general(
            toks[s], cots[s], (((0,), (0,)), ((), ())), preferred_element_type=jnp.float32
        )
        for s in range(replicas)
    ]
    entries = [
        jnp.sum(grads[s] * grads[t]) for s in range(replicas) for t in range(s, replicas)
    ]
    flat = lax.psum(jnp.stack(entries), ("rep", "mp"))
    at = {}
    k = 0
    for s in range(replicas):
        for t in range(s, replicas):
            at[s, t] = at[t, s] = k
            k += 1
    gram = jnp.stack(
        [jnp.stack([flat[at[s, t]] for t in range(replicas)]) for s in range(replicas)]
    )
    coef = mix(gram, replicas)
    update = coef[0] * grads[0]
    for s in range(1, replicas):
        update = update + coef[s] * grads[s]
    new_weight = (weight.astype(jnp.float32) - learning_rate * update).astype(jnp.bfloat16)
    product = jnp.dot(
        next_tokens,
        lax.all_gather(new_weight, "rep", axis=0, tiled=True),
        preferred_element_type=jnp.float32,
    )
    features = next_tokens.shape[1]
    next_query = (product * features ** (-0.5)).astype(jnp.bfloat16)
    return (new_weight, next_query)


def solution(mesh):
    in_specs = (P("rep", "mp"), P("rep", "mp"), P("rep", "mp"), P("rep", None))
    out_specs = (P("rep", "mp"), P("rep", "mp"))
    return jax.shard_map(local, mesh=mesh, in_specs=in_specs, out_specs=out_specs, check_vma=False)
```

```python
import functools

import jax
import jax.numpy as jnp
from jax import lax
from jax.experimental import pallas as pl
from jax.experimental.pallas import tpu as pltpu
from jax.sharding import PartitionSpec as P

learning_rate = 0.002
eps = 1e-06
MESH = pl.DeviceIdType.MESH
F32 = jnp.float32
BF16 = jnp.bfloat16


def ring_rep(position, n):
    back = lax.div(position, n // 2)
    return (1 - back) * (2 * position) + back * (2 * (n - 1 - position) + 1)


def ring_position(rep, n):
    odd = lax.rem(rep, 2)
    half = lax.div(rep, 2)
    return (1 - odd) * half + odd * (n - 1 - half)


def mix(entry, n):
    one = jnp.ones_like(entry[0, 0])
    members = [{s: one} for s in range(n)]
    gram = dict(entry)
    count = n
    while count > 1:
        mid = count // 2
        low, high = [], []
        for j in range(mid):
            cross = gram[j, j + mid]
            low.append(1.0 - cross / (2.0 * gram[j, j] + eps))
            high.append(1.0 - cross / (2.0 * gram[j + mid, j + mid] + eps))
        members = [
            {
                **{s: low[j] * v for s, v in members[j].items()},
                **{s: high[j] * v for s, v in members[j + mid].items()},
            }
            for j in range(mid)
        ]
        fresh = {}
        for j in range(mid):
            for k in range(j, mid):
                value = low[j] * (low[k] * gram[j, k] + high[k] * gram[j, k + mid])
                value += high[j] * (low[k] * gram[k, j + mid] + high[k] * gram[j + mid, k + mid])
                fresh[j, k] = value
        gram = fresh
        count = mid
    return [members[0][s] for s in range(n)]


def kernel(
    n, q, w_hbm, t_ref, c_ref, n_hbm,
    wnew, out,
    w_ref, t1, tfull, call, nfull, g, gacc, vown, vrep, vsum, vmp, sbuf, rbuf,
    loc, x1s, x1r, x2s, x2r, x3s, x3r, y2s, y2r, y3s, y3r, ags, agr, v1s, v1r, v2s, v2r, rss, rsr,
):
    per, width = c_ref.shape
    rows = w_ref.shape[0]
    quarter = per // q
    k = n // q
    half = width // 2
    H = n // 2
    r = lax.axis_index("rep")
    m = lax.axis_index("mp")
    p = ring_position(r, n)
    right = ring_rep(lax.rem(p + 1, n), n)
    left = ring_rep(lax.rem(p + n - 1, n), n)
    mine = pl.ds(pl.multiple_of(m * quarter, quarter), quarter)

    def rep_at(d):
        return lax.rem(r + d, n)

    def mp_at(d):
        return lax.rem(m + d, q)

    def remote(src, dst, ss, rs, rep, mp):
        return pltpu.make_async_remote_copy(
            src_ref=src, dst_ref=dst, send_sem=ss, recv_sem=rs, device_id=(rep, mp), device_id_type=MESH
        )

    w_copy = pltpu.make_async_copy(w_hbm, w_ref, loc.at[0])
    w_copy.start()
    c_copy = pltpu.make_async_copy(c_ref, call.at[r], loc.at[1])
    c_copy.start()
    t_copy = pltpu.make_async_copy(t_ref.at[mine], t1.at[m], loc.at[2])
    t_copy.start()

    barrier = pltpu.get_barrier_semaphore()
    for d in range(1, n):
        pl.semaphore_signal(barrier, inc=1, device_id=(rep_at(d), m), device_id_type=MESH)
    for d in range(1, q):
        pl.semaphore_signal(barrier, inc=1, device_id=(r, mp_at(d)), device_id_type=MESH)
    pl.semaphore_wait(barrier, n - 1 + q - 1)

    def first(d):
        peer = mp_at(d)
        src = t_ref.at[pl.ds(pl.multiple_of(peer * quarter, quarter), quarter)]
        return remote(src, t1.at[m], x1s.at[d], x1r.at[d], r, peer)

    def second_tokens(d):
        dest = rep_at(d)
        cols = pl.ds(pl.multiple_of(lax.rem(dest, k) * rows, rows), rows)
        src = t1.at[lax.div(dest, k), :, cols]
        return remote(src, tfull.at[r, mine], x2s.at[d], x2r.at[d], dest, m)

    def second_next(d):
        dest = rep_at(d)
        cols = pl.ds(pl.multiple_of(dest * rows, rows), rows)
        return remote(n_hbm.at[mine, cols], nfull.at[r, mine], y2s.at[d], y2r.at[d], dest, m)

    def third(buf, ss, rs, d):
        return remote(buf.at[:, mine], buf.at[:, mine], ss.at[d], rs.at[d], r, mp_at(d))

    def gather(way, c, j):
        shift = j * (1 - 2 * way)
        block = ring_rep(lax.rem(p + n - shift, n), n)
        ref = call.at[block, :, pl.ds(c * half, half)]
        return remote(ref, ref, ags.at[way, c, j], agr.at[way, c, j], (right, left)[way], m)

    def arrive(way, c, j):
        gather(way, c, j).wait_recv()

    def block_at(i):
        off = lax.div(i + 1, 2)
        side = 1 - 2 * lax.rem(i, 2)
        return ring_rep(lax.rem(p + n + side * off, n), n)

    rt = min(128, rows)
    gt = min(32, rows)

    def compute(i, _):
        s = block_at(i)

        for a in range(rows // rt):
            span = slice(a * rt, (a + 1) * rt)
            g[s, span, :] = lax.dot_general(
                tfull[s, :, span], call[s], (((0,), (0,)), ((), ())), preferred_element_type=F32
            )

        def pair(b, _):
            t = block_at(b)

            def chunk(a, sums):
                span = pl.ds(pl.multiple_of(a * gt, gt), gt)
                prod = g[s, span, :] * g[t, span, :]
                sums = list(sums)
                x = 0
                for u in range(gt // 8):
                    for v in range(width // 128):
                        sums[x % 4] = sums[x % 4] + prod[8 * u : 8 * u + 8, 128 * v : 128 * v + 128]
                        x += 1
                return tuple(sums)

            zero = jnp.zeros((8, 128), F32)
            a0, a1, a2, a3 = lax.fori_loop(0, rows // gt, chunk, (zero,) * 4)
            total = (a0 + a1) + (a2 + a3)
            gacc[s * n + t] = total
            gacc[t * n + s] = total
            return 0

        lax.fori_loop(0, i + 1, pair, 0)
        return 0

    for d in range(1, q):
        first(d).start()
    c_copy.wait()
    for c in range(2):
        for way in range(2):
            if H > 1 or c == way:
                gather(way, c, 0).start()
    t_copy.wait()
    for d in range(1, q):
        first(d).wait_recv()
    for d in range(1, n):
        second_tokens(d).start()
    own_cols = pl.ds(pl.multiple_of(lax.rem(r, k) * rows, rows), rows)
    own_t = pltpu.make_async_copy(t1.at[lax.div(r, k), :, own_cols], tfull.at[r, mine], loc.at[2])
    own_t.start()
    own_cols_n = pl.ds(pl.multiple_of(r * rows, rows), rows)
    own_n = pltpu.make_async_copy(n_hbm.at[mine, own_cols_n], nfull.at[r, mine], loc.at[3])
    own_n.start()

    def forward(j, _):
        for way, c in ((0, 0), (1, 1), (0, 1), (1, 0)):
            arrive(way, c, j - 1)
            gather(way, c, j).start()
        return 0

    lax.fori_loop(1, H - 2, forward, 0)
    own_t.wait()
    for d in range(1, n):
        second_tokens(d).wait_recv()
    for d in range(1, q):
        third(tfull, x3s, x3r, d).start()
    forward(H - 2, 0)
    for d in range(1, n):
        second_next(d).start()
    for d in range(1, q):
        third(tfull, x3s, x3r, d).wait_recv()
    lax.fori_loop(0, 2 * H - 3, compute, 0)
    for way, c in ((0, 0), (1, 1), (0, 1), (1, 0)):
        arrive(way, c, H - 2)
        if way == c:
            gather(way, c, H - 1).start()
    lax.fori_loop(2 * H - 3, 2 * H - 1, compute, 0)
    own_n.wait()
    for d in range(1, n):
        second_next(d).wait_recv()
    for d in range(1, q):
        third(nfull, y3s, y3r, d).start()
    for way in range(2):
        arrive(way, way, H - 1)
    compute(n - 1, 0)

    lane = lax.broadcasted_iota(jnp.int32, (n, 128), 1)
    sub = lax.broadcasted_iota(jnp.int32, (n, 128), 0)
    for s in range(n):
        part = jnp.sum(gacc[s * n : (s + 1) * n], axis=1)
        total = jnp.sum(part, axis=1, keepdims=True)
        vown[s : s + 1, :] = jnp.sum(jnp.where(lane == sub, total, 0.0), axis=0, keepdims=True)

    def over_rep(d):
        return remote(vown, vrep.at[d], v1s.at[d], v1r.at[d], rep_at(d), m)

    def over_mp(d):
        return remote(vsum, vmp.at[d], v2s.at[d], v2r.at[d], r, mp_at(d))

    for d in range(1, n):
        over_rep(d).start()
    acc = vown[...]
    for d in range(1, n):
        over_rep(d).wait_recv()
        acc = acc + vrep[d]
    vsum[...] = acc
    for d in range(1, q):
        over_mp(d).start()
    for d in range(1, q):
        over_mp(d).wait_recv()
        acc = acc + vmp[d]

    entry = {}
    lane1 = lax.broadcasted_iota(jnp.int32, (1, 128), 1)
    for s in range(n):
        for t in range(s, n):
            entry[s, t] = jnp.sum(jnp.where(lane1 == t, acc[s : s + 1, :], 0.0), axis=1, keepdims=True)
    coef = mix(entry, n)
    w_copy.wait()
    ct = min(64, rows)

    def combine(c):
        cols = slice(c * half, (c + 1) * half)

        def chunk(a, _):
            span = pl.ds(pl.multiple_of(a * ct, ct), ct)
            update = coef[0] * g[0, span, cols]
            for s in range(1, n):
                update = update + coef[s] * g[s, span, cols]
            wnew[span, cols] = (w_ref[span, cols].astype(F32) - learning_rate * update).astype(BF16)
            return 0

        lax.fori_loop(0, rows // ct, chunk, 0)

    def partial(block, c):
        return jnp.dot(nfull[block], wnew[:, c * half : (c + 1) * half], preferred_element_type=F32)

    def send(way, c, t):
        return remote(
            sbuf.at[way, c, t], rbuf.at[way, c, t], rss.at[way, c, t], rsr.at[way, c, t], (right, left)[way], m
        )

    def stage(way, c, t, add):
        shift = (H - t) * (1 - 2 * way)
        value = partial(ring_rep(lax.rem(p + n + shift, n), n), c)
        if add:
            send(way, c, t - 1).wait_recv()
            value = value + rbuf[way, c, t - 1].astype(F32)
        sbuf[way, c, t] = value.astype(BF16)
        send(way, c, t).start()

    combine(0)
    for d in range(1, q):
        third(nfull, y3s, y3r, d).wait_recv()
    stage(0, 0, 0, False)
    combine(1)
    stage(1, 1, 0, False)
    stage(0, 1, 1, False)
    stage(1, 0, 1, False)
    stage(0, 0, 1, True)
    stage(1, 1, 1, True)

    def step(t, _):
        for way, c in ((0, 1), (1, 0), (0, 0), (1, 1)):
            stage(way, c, t, True)
        return 0

    lax.fori_loop(2, H, step, 0)
    scale = n_hbm.shape[1] ** (-0.5)
    for c in range(2):
        value = partial(r, c)
        for way in (1 - c, c):
            send(way, c, H - 1).wait_recv()
            value = value + rbuf[way, c, H - 1].astype(F32)
        out[:, c * half : (c + 1) * half] = (value * scale).astype(BF16)

    for d in range(1, q):
        first(d).wait_send()
        third(tfull, x3s, x3r, d).wait_send()
        third(nfull, y3s, y3r, d).wait_send()
        over_mp(d).wait_send()
    for d in range(1, n):
        second_tokens(d).wait_send()
        second_next(d).wait_send()
        over_rep(d).wait_send()

    def drain(j, _):
        for way in range(2):
            for c in range(2):
                gather(way, c, j).wait_send()
                send(way, c, j + 1).wait_send()
        return 0

    lax.fori_loop(0, H - 1, drain, 0)
    for way in range(2):
        gather(way, way, H - 1).wait_send()
        send(way, way, 0).wait_send()


def local(n, q, weight, tokens, cotangent, next_tokens):
    rows, width = weight.shape
    per = cotangent.shape[0]
    H = n // 2
    dma = pltpu.SemaphoreType.DMA
    vm = pltpu.VMEM
    return pl.pallas_call(
        functools.partial(kernel, n, q),
        out_shape=(
            jax.ShapeDtypeStruct((rows, width), BF16),
            jax.ShapeDtypeStruct((per, width), BF16),
        ),
        in_specs=[
            pl.BlockSpec(memory_space=pl.ANY),
            pl.BlockSpec(memory_space=pltpu.VMEM),
            pl.BlockSpec(memory_space=pltpu.VMEM),
            pl.BlockSpec(memory_space=pl.ANY),
        ],
        out_specs=(pl.BlockSpec(memory_space=pltpu.VMEM), pl.BlockSpec(memory_space=pltpu.VMEM)),
        scratch_shapes=[
            vm((rows, width), BF16),
            vm((q, per // q, width), BF16),
            vm((n, per, rows), BF16),
            vm((n, per, width), BF16),
            vm((n, per, rows), BF16),
            vm((n, rows, width), F32),
            vm((n * n, 8, 128), F32),
            vm((n, 128), F32),
            vm((n, n, 128), F32),
            vm((n, 128), F32),
            vm((q, n, 128), F32),
            vm((2, 2, H, per, width // 2), BF16),
            vm((2, 2, H, per, width // 2), BF16),
            dma((4,)),
            dma((q,)), dma((q,)), dma((n,)), dma((n,)), dma((q,)), dma((q,)),
            dma((n,)), dma((n,)), dma((q,)), dma((q,)),
            dma((2, 2, H)), dma((2, 2, H)),
            dma((n,)), dma((n,)), dma((q,)), dma((q,)),
            dma((2, 2, H)), dma((2, 2, H)),
        ],
        compiler_params=pltpu.CompilerParams(
            collective_id=0, has_side_effects=True, vmem_limit_bytes=60 << 20
        ),
    )(weight, tokens, cotangent, next_tokens)


def solution(mesh):
    n, q = mesh.shape["rep"], mesh.shape["mp"]
    in_specs = (P("rep", "mp"), P("rep", "mp"), P("rep", "mp"), P("rep", None))
    out_specs = (P("rep", "mp"), P("rep", "mp"))
    return jax.shard_map(
        functools.partial(local, n, q), mesh=mesh, in_specs=in_specs, out_specs=out_specs, check_vma=False
    )
```

```python
import functools

import jax
import jax.numpy as jnp
from jax import lax
from jax.experimental import pallas as pl
from jax.experimental.pallas import tpu as pltpu
from jax.sharding import PartitionSpec as P

learning_rate = 0.002
eps = 1e-06
MESH = pl.DeviceIdType.MESH
F32 = jnp.float32
BF16 = jnp.bfloat16


def ring_rep(position, n):
    back = lax.div(position, n // 2)
    return (1 - back) * (2 * position) + back * (2 * (n - 1 - position) + 1)


def ring_position(rep, n):
    odd = lax.rem(rep, 2)
    half = lax.div(rep, 2)
    return (1 - odd) * half + odd * (n - 1 - half)


def mix(entry, n):
    one = jnp.ones_like(entry[0, 0])
    members = [{s: one} for s in range(n)]
    gram = dict(entry)
    count = n
    while count > 1:
        mid = count // 2
        low, high = [], []
        for j in range(mid):
            cross = gram[j, j + mid]
            low.append(1.0 - cross / (2.0 * gram[j, j] + eps))
            high.append(1.0 - cross / (2.0 * gram[j + mid, j + mid] + eps))
        members = [
            {
                **{s: low[j] * v for s, v in members[j].items()},
                **{s: high[j] * v for s, v in members[j + mid].items()},
            }
            for j in range(mid)
        ]
        fresh = {}
        for j in range(mid):
            for k in range(j, mid):
                value = low[j] * (low[k] * gram[j, k] + high[k] * gram[j, k + mid])
                value += high[j] * (low[k] * gram[k, j + mid] + high[k] * gram[j + mid, k + mid])
                fresh[j, k] = value
        gram = fresh
        count = mid
    return [members[0][s] for s in range(n)]


def kernel(
    n, q, w_hbm, t_hbm, c_hbm, n_hbm,
    w_out, q_out,
    wnew, out, w_ref, t1, tfull, call, nfull, g, gacc, vown, vrep, vsum, vmp, sbuf, rbuf,
    loc, x1s, x1r, x2s, x2r, x3s, x3r, y2s, y2r, y3s, y3r, zbs, zbr, ags, agr, v1s, v1r, v2s, v2r, rss, rsr,
):
    per, width = c_hbm.shape
    rows = w_ref.shape[0]
    quarter = per // q
    k = n // q
    half = width // 2
    H = n // 2
    order = [H]
    for a in range(1, H):
        order += [H + a, H - a]
    order += [0]
    r = lax.axis_index("rep")
    m = lax.axis_index("mp")
    p = ring_position(r, n)
    right = ring_rep(lax.rem(p + 1, n), n)
    left = ring_rep(lax.rem(p + n - 1, n), n)
    lines = q // 2
    core = lax.rem(m, 2)
    sibling = m + 1 - 2 * core

    def share(i):
        start = (lax.rem(i, 2) * lines + lax.div(i, 2)) * quarter
        return pl.ds(pl.multiple_of(start, quarter), quarter)

    mine = share(m)
    ours = pl.ds(pl.multiple_of(core * (per // 2), per // 2), per // 2)

    def rep_at(d):
        return lax.rem(r + d, n)

    def mp_at(d):
        return lax.rem(m + d, q)

    def remote(src, dst, ss, rs, rep, mp):
        return pltpu.make_async_remote_copy(
            src_ref=src, dst_ref=dst, send_sem=ss, recv_sem=rs, device_id=(rep, mp), device_id_type=MESH
        )

    w_copy = pltpu.make_async_copy(w_hbm, w_ref, loc.at[0])
    w_copy.start()
    c_copy = pltpu.make_async_copy(c_hbm, call.at[r], loc.at[1])
    c_copy.start()
    t_copy = pltpu.make_async_copy(t_hbm.at[mine], t1.at[m], loc.at[2])
    t_copy.start()

    barrier = pltpu.get_barrier_semaphore()
    for d in range(1, n):
        pl.semaphore_signal(barrier, inc=1, device_id=(rep_at(d), m), device_id_type=MESH)
    for d in range(1, q):
        pl.semaphore_signal(barrier, inc=1, device_id=(r, mp_at(d)), device_id_type=MESH)
    pl.semaphore_wait(barrier, n - 1 + q - 1)

    def first(d):
        peer = mp_at(d)
        return remote(t_hbm.at[share(peer)], t1.at[m], x1s.at[d], x1r.at[d], r, peer)

    def second_tokens(d):
        dest = rep_at(d)
        cols = pl.ds(pl.multiple_of(lax.rem(dest, k) * rows, rows), rows)
        src = t1.at[lax.div(dest, k), :, cols]
        return remote(src, tfull.at[r, mine], x2s.at[d], x2r.at[d], dest, m)

    def line_at(d):
        return lax.rem(lax.div(m, 2) + d, lines) * 2 + core

    def third(d):
        ref = tfull.at[:, mine]
        return remote(ref, ref, x3s.at[d], x3r.at[d], r, line_at(d))

    def fourth():
        ref = tfull.at[:, ours]
        return remote(ref, ref, x3s.at[0], x3r.at[0], r, sibling)

    def next_second(e):
        dest = ring_rep(lax.rem(p + e, n), n)
        cols = pl.ds(pl.multiple_of(dest * rows, rows), rows)
        return remote(n_hbm.at[mine, cols], nfull.at[r, mine], y2s.at[e], y2r.at[e], dest, m)

    def behind(e):
        return ring_rep(lax.rem(p + n - e, n), n)

    def next_third(e, d):
        ref = nfull.at[behind(e), mine]
        return remote(ref, ref, y3s.at[d, e], y3r.at[d, e], r, line_at(d))

    def next_fourth(e):
        ref = nfull.at[behind(e), ours]
        return remote(ref, ref, zbs.at[e], zbr.at[e], r, sibling)

    def gather(way, c, j):
        shift = j * (1 - 2 * way)
        block = ring_rep(lax.rem(p + n - shift, n), n)
        ref = call.at[block, :, pl.ds(c * half, half)]
        return remote(ref, ref, ags.at[way, c, j], agr.at[way, c, j], (right, left)[way], m)

    def arrive(way, c, j):
        gather(way, c, j).wait_recv()

    def block_at(i):
        off = lax.div(i + 1, 2)
        side = 1 - 2 * lax.rem(i, 2)
        return ring_rep(lax.rem(p + n + side * off, n), n)

    rt = min(128, rows)
    gt = min(64, rows)

    def compute(i, _):
        s = block_at(i)

        for a in range(rows // rt):
            span = slice(a * rt, (a + 1) * rt)
            g[s, span, :] = lax.dot_general(
                tfull[s, :, span], call[s], (((0,), (0,)), ((), ())), preferred_element_type=F32
            )

        def pairs(ts):
            def chunk(a, sums):
                span = pl.ds(pl.multiple_of(a * gt, gt), gt)
                sums = [list(x) for x in sums]
                x = 0
                for v in range(width // 128):
                    cols = slice(128 * v, 128 * v + 128)
                    base = g[s, span, cols]
                    for y, t in enumerate(ts):
                        prod = base * g[t, span, cols]
                        for u in range(gt // 8):
                            sums[y][u % 4] = sums[y][u % 4] + prod[8 * u : 8 * u + 8]
                return tuple(tuple(x) for x in sums)

            zero = jnp.zeros((8, 128), F32)
            sums = lax.fori_loop(0, rows // gt, chunk, ((zero,) * 4,) * len(ts))
            for t, (a0, a1, a2, a3) in zip(ts, sums):
                total = (a0 + a1) + (a2 + a3)
                gacc[s * n + t] = total
                gacc[t * n + s] = total

        def double(b, _):
            pairs([block_at(2 * b), block_at(2 * b + 1)])
            return 0

        def single(b, _):
            pairs([block_at(b)])
            return 0

        twos = lax.div(i + 1, 2)
        lax.fori_loop(0, twos, double, 0)
        lax.fori_loop(2 * twos, i + 1, single, 0)
        return 0

    for d in range(1, q):
        first(d).start()
    c_copy.wait()
    for c in range(2):
        for way in range(2):
            if H > 1 or c == way:
                gather(way, c, 0).start()
    t_copy.wait()
    for d in range(1, q):
        first(d).wait_recv()
    for d in range(1, n):
        second_tokens(d).start()
    own_cols = pl.ds(pl.multiple_of(lax.rem(r, k) * rows, rows), rows)
    own_t = pltpu.make_async_copy(t1.at[lax.div(r, k), :, own_cols], tfull.at[r, mine], loc.at[2])
    own_t.start()
    def forward(j, _):
        for way, c in ((0, 0), (1, 1), (0, 1), (1, 0)):
            arrive(way, c, j - 1)
            gather(way, c, j).start()
        return 0

    lax.fori_loop(1, H - 2, forward, 0)
    own_t.wait()
    for d in range(1, n):
        second_tokens(d).wait_recv()
    for d in range(1, lines):
        third(d).start()
    forward(H - 2, 0)
    for d in range(1, lines):
        third(d).wait_recv()
    fourth().start()
    fourth().wait_recv()
    lax.fori_loop(0, 3, compute, 0)
    for way, c in ((0, 0), (1, 1), (0, 1), (1, 0)):
        arrive(way, c, H - 2)
        if way == c:
            gather(way, c, H - 1).start()
    own_n = pltpu.make_async_copy(
        n_hbm.at[mine, pl.ds(pl.multiple_of(r * rows, rows), rows)], nfull.at[r, mine], loc.at[3]
    )
    own_n.start()
    lax.fori_loop(3, n - 1, compute, 0)
    for way in range(2):
        arrive(way, way, H - 1)
    compute(n - 1, 0)

    lane = lax.broadcasted_iota(jnp.int32, (n, 128), 1)
    sub = lax.broadcasted_iota(jnp.int32, (n, 128), 0)
    for s in range(n):
        part = jnp.sum(gacc[s * n : (s + 1) * n], axis=1)
        total = jnp.sum(part, axis=1, keepdims=True)
        vown[s : s + 1, :] = jnp.sum(jnp.where(lane == sub, total, 0.0), axis=0, keepdims=True)

    def over_rep(d):
        return remote(vown, vrep.at[d], v1s.at[d], v1r.at[d], rep_at(d), m)

    def over_mp(d):
        return remote(vsum, vmp.at[d], v2s.at[d], v2r.at[d], r, mp_at(d))

    for d in range(1, n):
        over_rep(d).start()
    for e in order[:-1]:
        next_second(e).start()
    acc = vown[...]
    for d in range(1, n):
        over_rep(d).wait_recv()
        acc = acc + vrep[d]
    vsum[...] = acc
    for d in range(1, q):
        over_mp(d).start()
    for d in range(1, q):
        over_mp(d).wait_recv()
        acc = acc + vmp[d]
    own_n.wait()
    for e in order:
        if e:
            next_second(e).wait_recv()
        for d in range(1, lines):
            next_third(e, d).start()

    entry = {}
    lane1 = lax.broadcasted_iota(jnp.int32, (1, 128), 1)
    for s in range(n):
        for t in range(s, n):
            entry[s, t] = jnp.sum(jnp.where(lane1 == t, acc[s : s + 1, :], 0.0), axis=1, keepdims=True)
    coef = mix(entry, n)
    w_copy.wait()
    ct = min(64, rows)

    def combine(c):
        cols = slice(c * half, (c + 1) * half)

        def chunk(a, _):
            span = pl.ds(pl.multiple_of(a * ct, ct), ct)
            update = coef[0] * g[0, span, cols]
            for s in range(1, n):
                update = update + coef[s] * g[s, span, cols]
            wnew[span, cols] = (w_ref[span, cols].astype(F32) - learning_rate * update).astype(BF16)
            return 0

        lax.fori_loop(0, rows // ct, chunk, 0)

    def partial(block, c):
        return jnp.dot(nfull[block], wnew[:, c * half : (c + 1) * half], preferred_element_type=F32)

    def send(way, c, t):
        return remote(
            sbuf.at[way, c, t], rbuf.at[way, c, t], rss.at[way, c, t], rsr.at[way, c, t], (right, left)[way], m
        )

    def stage(way, c, t, add):
        shift = (H - t) * (1 - 2 * way)
        value = partial(ring_rep(lax.rem(p + n + shift, n), n), c)
        if add:
            send(way, c, t - 1).wait_recv()
            value = value + rbuf[way, c, t - 1].astype(F32)
        sbuf[way, c, t] = value.astype(BF16)
        send(way, c, t).start()

    combine(0)
    for d in range(1, lines):
        next_third(H, d).wait_recv()
    next_fourth(H).start()
    next_fourth(H).wait_recv()
    stage(0, 0, 0, False)
    combine(1)
    w_back = pltpu.make_async_copy(wnew, w_out, loc.at[0])
    w_back.start()
    stage(1, 1, 0, False)
    for e in order[1:]:
        for d in range(1, lines):
            next_third(e, d).wait_recv()
        next_fourth(e).start()
    for e in order[1:]:
        next_fourth(e).wait_recv()
    stage(0, 1, 1, False)
    stage(1, 0, 1, False)
    stage(0, 0, 1, True)
    stage(1, 1, 1, True)

    def step(t, _):
        for way, c in ((0, 1), (1, 0), (0, 0), (1, 1)):
            stage(way, c, t, True)
        return 0

    lax.fori_loop(2, H, step, 0)
    scale = n_hbm.shape[1] ** (-0.5)
    for c in range(2):
        value = partial(r, c)
        for way in (1 - c, c):
            send(way, c, H - 1).wait_recv()
            value = value + rbuf[way, c, H - 1].astype(F32)
        out[:, c * half : (c + 1) * half] = (value * scale).astype(BF16)

    back = pltpu.make_async_copy(out, q_out, loc.at[1])
    back.start()
    for d in range(1, q):
        first(d).wait_send()
        over_mp(d).wait_send()
    for d in range(1, lines):
        third(d).wait_send()
        for e in range(n):
            next_third(e, d).wait_send()
    fourth().wait_send()
    for e in range(n):
        next_fourth(e).wait_send()
    for d in range(1, n):
        second_tokens(d).wait_send()
        next_second(d).wait_send()
        over_rep(d).wait_send()

    def drain(j, _):
        for way in range(2):
            for c in range(2):
                gather(way, c, j).wait_send()
                send(way, c, j + 1).wait_send()
        return 0

    lax.fori_loop(0, H - 1, drain, 0)
    for way in range(2):
        gather(way, way, H - 1).wait_send()
        send(way, way, 0).wait_send()
    w_back.wait()
    back.wait()


def local(n, q, weight, tokens, cotangent, next_tokens):
    rows, width = weight.shape
    per = cotangent.shape[0]
    H = n // 2
    dma = pltpu.SemaphoreType.DMA
    vm = pltpu.VMEM
    return pl.pallas_call(
        functools.partial(kernel, n, q),
        out_shape=(
            jax.ShapeDtypeStruct((rows, width), BF16),
            jax.ShapeDtypeStruct((per, width), BF16),
        ),
        in_specs=[
            pl.BlockSpec(memory_space=pl.ANY) for _ in range(4)
        ],
        out_specs=(pl.BlockSpec(memory_space=pl.ANY), pl.BlockSpec(memory_space=pl.ANY)),
        scratch_shapes=[
            vm((rows, width), BF16),
            vm((per, width), BF16),
            vm((rows, width), BF16),
            vm((q, per // q, width), BF16),
            vm((n, per, rows), BF16),
            vm((n, per, width), BF16),
            vm((n, per, rows), BF16),
            vm((n, rows, width), F32),
            vm((n * n, 8, 128), F32),
            vm((n, 128), F32),
            vm((n, n, 128), F32),
            vm((n, 128), F32),
            vm((q, n, 128), F32),
            vm((2, 2, H, per, width // 2), BF16),
            vm((2, 2, H, per, width // 2), BF16),
            dma((4,)),
            dma((q,)), dma((q,)), dma((n,)), dma((n,)), dma((q,)), dma((q,)),
            dma((n,)), dma((n,)), dma((q // 2, n)), dma((q // 2, n)), dma((n,)), dma((n,)),
            dma((2, 2, H)), dma((2, 2, H)),
            dma((n,)), dma((n,)), dma((q,)), dma((q,)),
            dma((2, 2, H)), dma((2, 2, H)),
        ],
        compiler_params=pltpu.CompilerParams(
            collective_id=0, has_side_effects=True, vmem_limit_bytes=60 << 20
        ),
    )(weight, tokens, cotangent, next_tokens)


def solution(mesh):
    n, q = mesh.shape["rep"], mesh.shape["mp"]
    in_specs = (P("rep", "mp"), P("rep", "mp"), P("rep", "mp"), P("rep", None))
    out_specs = (P("rep", "mp"), P("rep", "mp"))
    return jax.shard_map(
        functools.partial(local, n, q), mesh=mesh, in_specs=in_specs, out_specs=out_specs, check_vma=False
    )
```

```python
import functools

import jax
import jax.numpy as jnp
from jax import lax
from jax.experimental import pallas as pl
from jax.experimental.pallas import tpu as pltpu
from jax.sharding import PartitionSpec as P

learning_rate = 0.002
eps = 1e-06
MESH = pl.DeviceIdType.MESH
F32 = jnp.float32
BF16 = jnp.bfloat16


def ring_rep(position, n):
    back = lax.div(position, n // 2)
    return (1 - back) * (2 * position) + back * (2 * (n - 1 - position) + 1)


def ring_position(rep, n):
    odd = lax.rem(rep, 2)
    half = lax.div(rep, 2)
    return (1 - odd) * half + odd * (n - 1 - half)


def mix(entry, n):
    one = jnp.ones_like(entry[0, 0])
    members = [{s: one} for s in range(n)]
    gram = dict(entry)
    count = n
    while count > 1:
        mid = count // 2
        low, high = [], []
        for j in range(mid):
            cross = gram[j, j + mid]
            low.append(1.0 - cross / (2.0 * gram[j, j] + eps))
            high.append(1.0 - cross / (2.0 * gram[j + mid, j + mid] + eps))
        members = [
            {
                **{s: low[j] * v for s, v in members[j].items()},
                **{s: high[j] * v for s, v in members[j + mid].items()},
            }
            for j in range(mid)
        ]
        fresh = {}
        for j in range(mid):
            for k in range(j, mid):
                value = low[j] * (low[k] * gram[j, k] + high[k] * gram[j, k + mid])
                value += high[j] * (low[k] * gram[k, j + mid] + high[k] * gram[j + mid, k + mid])
                fresh[j, k] = value
        gram = fresh
        count = mid
    return [members[0][s] for s in range(n)]


def kernel(
    n, q, w_hbm, t_hbm, c_hbm, n_hbm,
    w_out, q_out,
    wnew, out, w_ref, t1, tfull, call, nfull, g, gacc, vown, vrep, vsum, vmp, sbuf, rbuf,
    loc, x1s, x1r, x2s, x2r, x3s, x3r, y2s, y2r, y3s, y3r, zbs, zbr, ags, agr, v1s, v1r, v2s, v2r, rss, rsr,
):
    per, width = c_hbm.shape
    rows = w_ref.shape[0]
    quarter = per // q
    k = n // q
    half = width // 2
    H = n // 2
    order = [H]
    for a in range(1, H):
        order += [H + a, H - a]
    order += [0]
    r = lax.axis_index("rep")
    m = lax.axis_index("mp")
    p = ring_position(r, n)
    right = ring_rep(lax.rem(p + 1, n), n)
    left = ring_rep(lax.rem(p + n - 1, n), n)
    lines = q // 2
    core = lax.rem(m, 2)
    sibling = m + 1 - 2 * core

    def share(i):
        start = (lax.rem(i, 2) * lines + lax.div(i, 2)) * quarter
        return pl.ds(pl.multiple_of(start, quarter), quarter)

    mine = share(m)
    ours = pl.ds(pl.multiple_of(core * (per // 2), per // 2), per // 2)

    def rep_at(d):
        return lax.rem(r + d, n)

    def mp_at(d):
        return lax.rem(m + d, q)

    def remote(src, dst, ss, rs, rep, mp):
        return pltpu.make_async_remote_copy(
            src_ref=src, dst_ref=dst, send_sem=ss, recv_sem=rs, device_id=(rep, mp), device_id_type=MESH
        )

    w_copy = pltpu.make_async_copy(w_hbm, w_ref, loc.at[0])
    w_copy.start()
    c_copy = pltpu.make_async_copy(c_hbm, call.at[r], loc.at[1])
    c_copy.start()
    t_copy = pltpu.make_async_copy(t_hbm.at[mine], t1.at[m], loc.at[2])
    t_copy.start()

    barrier = pltpu.get_barrier_semaphore()
    for d in range(1, n):
        pl.semaphore_signal(barrier, inc=1, device_id=(rep_at(d), m), device_id_type=MESH)
    for d in range(1, q):
        pl.semaphore_signal(barrier, inc=1, device_id=(r, mp_at(d)), device_id_type=MESH)
    pl.semaphore_wait(barrier, n - 1 + q - 1)

    def first(d):
        peer = mp_at(d)
        return remote(t_hbm.at[share(peer)], t1.at[m], x1s.at[d], x1r.at[d], r, peer)

    def second_tokens(d):
        dest = rep_at(d)
        cols = pl.ds(pl.multiple_of(lax.rem(dest, k) * rows, rows), rows)
        src = t1.at[lax.div(dest, k), :, cols]
        return remote(src, tfull.at[r, mine], x2s.at[d], x2r.at[d], dest, m)

    def line_at(d):
        return lax.rem(lax.div(m, 2) + d, lines) * 2 + core

    def third(d):
        ref = tfull.at[:, mine]
        return remote(ref, ref, x3s.at[d], x3r.at[d], r, line_at(d))

    def fourth():
        ref = tfull.at[:, ours]
        return remote(ref, ref, x3s.at[0], x3r.at[0], r, sibling)

    def next_second(e):
        dest = ring_rep(lax.rem(p + e, n), n)
        cols = pl.ds(pl.multiple_of(dest * rows, rows), rows)
        return remote(n_hbm.at[mine, cols], nfull.at[r, mine], y2s.at[e], y2r.at[e], dest, m)

    def behind(e):
        return ring_rep(lax.rem(p + n - e, n), n)

    def next_third(e, d):
        ref = nfull.at[behind(e), mine]
        return remote(ref, ref, y3s.at[d, e], y3r.at[d, e], r, line_at(d))

    def next_fourth(e):
        ref = nfull.at[behind(e), ours]
        return remote(ref, ref, zbs.at[e], zbr.at[e], r, sibling)

    def gather(way, c, j):
        shift = j * (1 - 2 * way)
        block = ring_rep(lax.rem(p + n - shift, n), n)
        ref = call.at[block, :, pl.ds(c * half, half)]
        return remote(ref, ref, ags.at[way, c, j], agr.at[way, c, j], (right, left)[way], m)

    def arrive(way, c, j):
        gather(way, c, j).wait_recv()

    def block_at(i):
        off = lax.div(i + 1, 2)
        side = 1 - 2 * lax.rem(i, 2)
        return ring_rep(lax.rem(p + n + side * off, n), n)

    rt = min(128, rows)
    gt = min(64, rows)

    def compute(i, _):
        s = block_at(i)

        for a in range(rows // rt):
            span = slice(a * rt, (a + 1) * rt)
            g[s, span, :] = lax.dot_general(
                tfull[s, :, span], call[s], (((0,), (0,)), ((), ())), preferred_element_type=F32
            )

        def pairs(ts):
            def chunk(a, sums):
                span = pl.ds(pl.multiple_of(a * gt, gt), gt)
                sums = [list(x) for x in sums]
                x = 0
                for v in range(width // 128):
                    cols = slice(128 * v, 128 * v + 128)
                    base = g[s, span, cols]
                    for y, t in enumerate(ts):
                        prod = base * g[t, span, cols]
                        for u in range(gt // 8):
                            sums[y][u % 4] = sums[y][u % 4] + prod[8 * u : 8 * u + 8]
                return tuple(tuple(x) for x in sums)

            zero = jnp.zeros((8, 128), F32)
            sums = lax.fori_loop(0, rows // gt, chunk, ((zero,) * 4,) * len(ts))
            for t, (a0, a1, a2, a3) in zip(ts, sums):
                total = (a0 + a1) + (a2 + a3)
                gacc[s * n + t] = total
                gacc[t * n + s] = total

        def double(b, _):
            pairs([block_at(2 * b), block_at(2 * b + 1)])
            return 0

        def single(b, _):
            pairs([block_at(b)])
            return 0

        twos = lax.div(i + 1, 2)
        lax.fori_loop(0, twos, double, 0)
        lax.fori_loop(2 * twos, i + 1, single, 0)
        return 0

    for d in range(1, q):
        first(d).start()
    c_copy.wait()
    for c in range(2):
        for way in range(2):
            if H > 1 or c == way:
                gather(way, c, 0).start()
    t_copy.wait()
    for d in range(1, q):
        first(d).wait_recv()
    for d in range(1, n):
        second_tokens(d).start()
    own_cols = pl.ds(pl.multiple_of(lax.rem(r, k) * rows, rows), rows)
    own_t = pltpu.make_async_copy(t1.at[lax.div(r, k), :, own_cols], tfull.at[r, mine], loc.at[2])
    own_t.start()
    def forward(j, _):
        for way, c in ((0, 0), (1, 1), (0, 1), (1, 0)):
            arrive(way, c, j - 1)
            gather(way, c, j).start()
        return 0

    lax.fori_loop(1, H - 2, forward, 0)
    own_t.wait()
    for d in range(1, n):
        second_tokens(d).wait_recv()
    for d in range(1, lines):
        third(d).start()
    forward(H - 2, 0)
    for d in range(1, lines):
        third(d).wait_recv()
    fourth().start()
    fourth().wait_recv()
    lax.fori_loop(0, 3, compute, 0)
    for way, c in ((0, 0), (1, 1), (0, 1), (1, 0)):
        arrive(way, c, H - 2)
        if way == c:
            gather(way, c, H - 1).start()
    own_n = pltpu.make_async_copy(
        n_hbm.at[mine, pl.ds(pl.multiple_of(r * rows, rows), rows)], nfull.at[r, mine], loc.at[3]
    )
    own_n.start()
    lax.fori_loop(3, n - 1, compute, 0)
    for way in range(2):
        arrive(way, way, H - 1)
    early = 3
    for e in order[:early]:
        next_second(e).start()
    compute(n - 1, 0)

    lane = lax.broadcasted_iota(jnp.int32, (n, 128), 1)
    sub = lax.broadcasted_iota(jnp.int32, (n, 128), 0)
    for s in range(n):
        part = jnp.sum(gacc[s * n : (s + 1) * n], axis=1)
        total = jnp.sum(part, axis=1, keepdims=True)
        vown[s : s + 1, :] = jnp.sum(jnp.where(lane == sub, total, 0.0), axis=0, keepdims=True)

    def over_rep(d):
        return remote(vown, vrep.at[d], v1s.at[d], v1r.at[d], rep_at(d), m)

    def over_mp(d):
        return remote(vsum, vmp.at[d], v2s.at[d], v2r.at[d], r, mp_at(d))

    for d in range(1, n):
        over_rep(d).start()
    for e in order[early:-1]:
        next_second(e).start()
    acc = vown[...]
    for d in range(1, n):
        over_rep(d).wait_recv()
        acc = acc + vrep[d]
    vsum[...] = acc
    for d in range(1, q):
        over_mp(d).start()
    own_n.wait()

    def pass_on(es):
        for e in es:
            if e:
                next_second(e).wait_recv()
            for d in range(1, lines):
                next_third(e, d).start()

    def share_chip(es):
        for e in es:
            for d in range(1, lines):
                next_third(e, d).wait_recv()
            next_fourth(e).start()

    def ready(es):
        for e in es:
            next_fourth(e).wait_recv()

    pass_on(order[:1])
    for d in range(1, q):
        over_mp(d).wait_recv()
        acc = acc + vmp[d]
    pass_on(order[1:early])

    entry = {}
    lane1 = lax.broadcasted_iota(jnp.int32, (1, 128), 1)
    for s in range(n):
        for t in range(s, n):
            entry[s, t] = jnp.sum(jnp.where(lane1 == t, acc[s : s + 1, :], 0.0), axis=1, keepdims=True)
    coef = mix(entry, n)
    w_copy.wait()
    ct = min(64, rows)

    def combine(c):
        cols = slice(c * half, (c + 1) * half)

        def chunk(a, _):
            span = pl.ds(pl.multiple_of(a * ct, ct), ct)
            update = coef[0] * g[0, span, cols]
            for s in range(1, n):
                update = update + coef[s] * g[s, span, cols]
            wnew[span, cols] = (w_ref[span, cols].astype(F32) - learning_rate * update).astype(BF16)
            return 0

        lax.fori_loop(0, rows // ct, chunk, 0)

    def partial(block, c):
        return jnp.dot(nfull[block], wnew[:, c * half : (c + 1) * half], preferred_element_type=F32)

    def send(way, c, t):
        return remote(
            sbuf.at[way, c, t], rbuf.at[way, c, t], rss.at[way, c, t], rsr.at[way, c, t], (right, left)[way], m
        )

    def stage(way, c, t, add):
        shift = (H - t) * (1 - 2 * way)
        value = partial(ring_rep(lax.rem(p + n + shift, n), n), c)
        if add:
            send(way, c, t - 1).wait_recv()
            value = value + rbuf[way, c, t - 1].astype(F32)
        sbuf[way, c, t] = value.astype(BF16)
        send(way, c, t).start()

    combine(0)
    share_chip(order[:1])
    pass_on(order[early : early + 2])
    combine(1)
    w_back = pltpu.make_async_copy(wnew, w_out, loc.at[0])
    w_back.start()
    ready(order[:1])
    stage(0, 0, 0, False)
    stage(1, 1, 0, False)
    pass_on(order[early + 2 :])
    share_chip(order[1:early])
    for t in range(1, H):
        if t + 1 < H:
            share_chip(order[2 * t + 1 : 2 * t + 3])
        else:
            share_chip(order[2 * t + 1 :])
        ready(order[2 * t - 1 : 2 * t + 1])
        for way, c in ((0, 1), (1, 0), (0, 0), (1, 1)):
            stage(way, c, t, t > 1 or way == c)
    ready(order[-1:])
    scale = n_hbm.shape[1] ** (-0.5)
    for c in range(2):
        value = partial(r, c)
        for way in (1 - c, c):
            send(way, c, H - 1).wait_recv()
            value = value + rbuf[way, c, H - 1].astype(F32)
        out[:, c * half : (c + 1) * half] = (value * scale).astype(BF16)

    back = pltpu.make_async_copy(out, q_out, loc.at[1])
    back.start()
    for d in range(1, q):
        first(d).wait_send()
        over_mp(d).wait_send()
    for d in range(1, lines):
        third(d).wait_send()
        for e in range(n):
            next_third(e, d).wait_send()
    fourth().wait_send()
    for e in range(n):
        next_fourth(e).wait_send()
    for d in range(1, n):
        second_tokens(d).wait_send()
        next_second(d).wait_send()
        over_rep(d).wait_send()

    def drain(j, _):
        for way in range(2):
            for c in range(2):
                gather(way, c, j).wait_send()
                send(way, c, j + 1).wait_send()
        return 0

    lax.fori_loop(0, H - 1, drain, 0)
    for way in range(2):
        gather(way, way, H - 1).wait_send()
        send(way, way, 0).wait_send()
    w_back.wait()
    back.wait()


def local(n, q, weight, tokens, cotangent, next_tokens):
    rows, width = weight.shape
    per = cotangent.shape[0]
    H = n // 2
    dma = pltpu.SemaphoreType.DMA
    vm = pltpu.VMEM
    return pl.pallas_call(
        functools.partial(kernel, n, q),
        out_shape=(
            pltpu.VMEM((rows, width), BF16),
            pltpu.VMEM((per, width), BF16),
        ),
        in_specs=[
            pl.BlockSpec(memory_space=pl.ANY) for _ in range(4)
        ],
        out_specs=(pl.BlockSpec(memory_space=pltpu.VMEM), pl.BlockSpec(memory_space=pltpu.VMEM)),
        scratch_shapes=[
            vm((rows, width), BF16),
            vm((per, width), BF16),
            vm((rows, width), BF16),
            vm((q, per // q, width), BF16),
            vm((n, per, rows), BF16),
            vm((n, per, width), BF16),
            vm((n, per, rows), BF16),
            vm((n, rows, width), F32),
            vm((n * n, 8, 128), F32),
            vm((n, 128), F32),
            vm((n, n, 128), F32),
            vm((n, 128), F32),
            vm((q, n, 128), F32),
            vm((2, 2, H, per, width // 2), BF16),
            vm((2, 2, H, per, width // 2), BF16),
            dma((4,)),
            dma((q,)), dma((q,)), dma((n,)), dma((n,)), dma((q,)), dma((q,)),
            dma((n,)), dma((n,)), dma((q // 2, n)), dma((q // 2, n)), dma((n,)), dma((n,)),
            dma((2, 2, H)), dma((2, 2, H)),
            dma((n,)), dma((n,)), dma((q,)), dma((q,)),
            dma((2, 2, H)), dma((2, 2, H)),
        ],
        compiler_params=pltpu.CompilerParams(
            collective_id=0, has_side_effects=True, vmem_limit_bytes=62 << 20
        ),
    )(weight, tokens, cotangent, next_tokens)


def solution(mesh):
    n, q = mesh.shape["rep"], mesh.shape["mp"]
    in_specs = (P("rep", "mp"), P("rep", "mp"), P("rep", "mp"), P("rep", None))
    out_specs = (P("rep", "mp"), P("rep", "mp"))
    return jax.shard_map(
        functools.partial(local, n, q), mesh=mesh, in_specs=in_specs, out_specs=out_specs, check_vma=False
    )
```

```python
import functools

import jax
import jax.numpy as jnp
from jax import lax
from jax.experimental import pallas as pl
from jax.experimental.pallas import tpu as pltpu
from jax.sharding import PartitionSpec as P

learning_rate = 0.002
eps = 1e-06
MESH = pl.DeviceIdType.MESH
F32 = jnp.float32
BF16 = jnp.bfloat16


def ring_rep(position, n):
    back = lax.div(position, n // 2)
    return (1 - back) * (2 * position) + back * (2 * (n - 1 - position) + 1)


def ring_position(rep, n):
    odd = lax.rem(rep, 2)
    half = lax.div(rep, 2)
    return (1 - odd) * half + odd * (n - 1 - half)


def mix(entry, n):
    one = jnp.ones_like(entry[0, 0])
    members = [{s: one} for s in range(n)]
    gram = dict(entry)
    count = n
    while count > 1:
        mid = count // 2
        low, high = [], []
        for j in range(mid):
            cross = gram[j, j + mid]
            low.append(1.0 - cross / (2.0 * gram[j, j] + eps))
            high.append(1.0 - cross / (2.0 * gram[j + mid, j + mid] + eps))
        members = [
            {
                **{s: low[j] * v for s, v in members[j].items()},
                **{s: high[j] * v for s, v in members[j + mid].items()},
            }
            for j in range(mid)
        ]
        fresh = {}
        for j in range(mid):
            for k in range(j, mid):
                value = low[j] * (low[k] * gram[j, k] + high[k] * gram[j, k + mid])
                value += high[j] * (low[k] * gram[k, j + mid] + high[k] * gram[j + mid, k + mid])
                fresh[j, k] = value
        gram = fresh
        count = mid
    return [members[0][s] for s in range(n)]


def kernel(
    n, q, w_hbm, t_hbm, c_hbm, n_hbm,
    w_out, q_out,
    wnew, out, w_ref, t1, tfull, call, nfull, g, gacc, vown, vrep, vsum, vmp, sbuf, rbuf,
    loc, x1s, x1r, x2s, x2r, x3s, x3r, y2s, y2r, y3s, y3r, zbs, zbr, ags, agr, v1s, v1r, v2s, v2r, rss, rsr,
):
    per, width = c_hbm.shape
    rows = w_ref.shape[0]
    quarter = per // q
    k = n // q
    half = width // 2
    H = n // 2
    order = [H]
    for a in range(1, H):
        order += [H + a, H - a]
    order += [0]
    r = lax.axis_index("rep")
    m = lax.axis_index("mp")
    p = ring_position(r, n)
    right = ring_rep(lax.rem(p + 1, n), n)
    left = ring_rep(lax.rem(p + n - 1, n), n)
    lines = q // 2
    core = lax.rem(m, 2)
    sibling = m + 1 - 2 * core

    def share(i):
        start = (lax.rem(i, 2) * lines + lax.div(i, 2)) * quarter
        return pl.ds(pl.multiple_of(start, quarter), quarter)

    mine = share(m)
    ours = pl.ds(pl.multiple_of(core * (per // 2), per // 2), per // 2)

    def rep_at(d):
        return lax.rem(r + d, n)

    def mp_at(d):
        return lax.rem(m + d, q)

    def remote(src, dst, ss, rs, rep, mp):
        return pltpu.make_async_remote_copy(
            src_ref=src, dst_ref=dst, send_sem=ss, recv_sem=rs, device_id=(rep, mp), device_id_type=MESH
        )

    w_copy = pltpu.make_async_copy(w_hbm, w_ref, loc.at[0])
    w_copy.start()
    c_copy = pltpu.make_async_copy(c_hbm, call.at[r], loc.at[1])
    c_copy.start()
    t_copy = pltpu.make_async_copy(t_hbm.at[mine], t1.at[m], loc.at[2])
    t_copy.start()

    barrier = pltpu.get_barrier_semaphore()
    for d in range(1, n):
        pl.semaphore_signal(barrier, inc=1, device_id=(rep_at(d), m), device_id_type=MESH)
    for d in range(1, q):
        pl.semaphore_signal(barrier, inc=1, device_id=(r, mp_at(d)), device_id_type=MESH)
    pl.semaphore_wait(barrier, n - 1 + q - 1)

    def first(d):
        peer = mp_at(d)
        return remote(t_hbm.at[share(peer)], t1.at[m], x1s.at[d], x1r.at[d], r, peer)

    def second_tokens(d):
        dest = rep_at(d)
        cols = pl.ds(pl.multiple_of(lax.rem(dest, k) * rows, rows), rows)
        src = t1.at[lax.div(dest, k), :, cols]
        return remote(src, tfull.at[r, mine], x2s.at[d], x2r.at[d], dest, m)

    def line_at(d):
        return lax.rem(lax.div(m, 2) + d, lines) * 2 + core

    def third(d):
        ref = tfull.at[:, mine]
        return remote(ref, ref, x3s.at[d], x3r.at[d], r, line_at(d))

    def fourth():
        ref = tfull.at[:, ours]
        return remote(ref, ref, x3s.at[0], x3r.at[0], r, sibling)

    def next_second(e):
        dest = ring_rep(lax.rem(p + e, n), n)
        cols = pl.ds(pl.multiple_of(dest * rows, rows), rows)
        return remote(n_hbm.at[mine, cols], nfull.at[r, mine], y2s.at[e], y2r.at[e], dest, m)

    def behind(e):
        return ring_rep(lax.rem(p + n - e, n), n)

    def next_third(e, d):
        ref = nfull.at[behind(e), mine]
        return remote(ref, ref, y3s.at[d, e], y3r.at[d, e], r, line_at(d))

    def next_fourth(e):
        ref = nfull.at[behind(e), ours]
        return remote(ref, ref, zbs.at[e], zbr.at[e], r, sibling)

    def gather(way, c, j):
        shift = j * (1 - 2 * way)
        block = ring_rep(lax.rem(p + n - shift, n), n)
        ref = call.at[block, :, pl.ds(c * half, half)]
        return remote(ref, ref, ags.at[way, c, j], agr.at[way, c, j], (right, left)[way], m)

    def arrive(way, c, j):
        gather(way, c, j).wait_recv()

    def block_at(i):
        off = lax.div(i + 1, 2)
        side = 1 - 2 * lax.rem(i, 2)
        return ring_rep(lax.rem(p + n + side * off, n), n)

    rt = min(128, rows)
    gt = min(128, rows)

    def compute(i, _):
        s = block_at(i)

        for a in range(rows // rt):
            span = slice(a * rt, (a + 1) * rt)
            g[s, span, :] = lax.dot_general(
                tfull[s, :, span], call[s], (((0,), (0,)), ((), ())), preferred_element_type=F32
            )

        def pairs(ts):
            def chunk(a, sums):
                span = pl.ds(pl.multiple_of(a * gt, gt), gt)
                sums = [list(x) for x in sums]
                x = 0
                for v in range(width // 128):
                    cols = slice(128 * v, 128 * v + 128)
                    base = g[s, span, cols]
                    for y, t in enumerate(ts):
                        prod = base * g[t, span, cols]
                        for u in range(gt // 8):
                            sums[y][u % 4] = sums[y][u % 4] + prod[8 * u : 8 * u + 8]
                return tuple(tuple(x) for x in sums)

            zero = jnp.zeros((8, 128), F32)
            sums = lax.fori_loop(0, rows // gt, chunk, ((zero,) * 4,) * len(ts))
            for t, (a0, a1, a2, a3) in zip(ts, sums):
                total = (a0 + a1) + (a2 + a3)
                gacc[s * n + t] = total
                gacc[t * n + s] = total

        def double(b, _):
            pairs([block_at(2 * b), block_at(2 * b + 1)])
            return 0

        def single(b, _):
            pairs([block_at(b)])
            return 0

        twos = lax.div(i + 1, 2)
        lax.fori_loop(0, twos, double, 0)
        lax.fori_loop(2 * twos, i + 1, single, 0)
        return 0

    for d in range(1, q):
        first(d).start()
    c_copy.wait()
    for c in range(2):
        for way in range(2):
            if H > 1 or c == way:
                gather(way, c, 0).start()
    t_copy.wait()
    for d in range(1, q):
        first(d).wait_recv()
    for d in range(1, n):
        second_tokens(d).start()
    own_cols = pl.ds(pl.multiple_of(lax.rem(r, k) * rows, rows), rows)
    own_t = pltpu.make_async_copy(t1.at[lax.div(r, k), :, own_cols], tfull.at[r, mine], loc.at[2])
    own_t.start()
    def forward(j, _):
        for way, c in ((0, 0), (1, 1), (0, 1), (1, 0)):
            arrive(way, c, j - 1)
            gather(way, c, j).start()
        return 0

    lax.fori_loop(1, H - 2, forward, 0)
    own_t.wait()
    for d in range(1, n):
        second_tokens(d).wait_recv()
    for d in range(1, lines):
        third(d).start()
    forward(H - 2, 0)
    for d in range(1, lines):
        third(d).wait_recv()
    fourth().start()
    fourth().wait_recv()
    lax.fori_loop(0, 3, compute, 0)
    for way, c in ((0, 0), (1, 1), (0, 1), (1, 0)):
        arrive(way, c, H - 2)
        if way == c:
            gather(way, c, H - 1).start()
    own_n = pltpu.make_async_copy(
        n_hbm.at[mine, pl.ds(pl.multiple_of(r * rows, rows), rows)], nfull.at[r, mine], loc.at[3]
    )
    own_n.start()
    lax.fori_loop(3, n - 1, compute, 0)
    for way in range(2):
        arrive(way, way, H - 1)
    early = 3
    for e in order[:early]:
        next_second(e).start()
    compute(n - 1, 0)

    lane = lax.broadcasted_iota(jnp.int32, (n, 128), 1)
    sub = lax.broadcasted_iota(jnp.int32, (n, 128), 0)
    for s in range(n):
        part = jnp.sum(gacc[s * n : (s + 1) * n], axis=1)
        total = jnp.sum(part, axis=1, keepdims=True)
        vown[s : s + 1, :] = jnp.sum(jnp.where(lane == sub, total, 0.0), axis=0, keepdims=True)

    def over_rep(d):
        return remote(vown, vrep.at[d], v1s.at[d], v1r.at[d], rep_at(d), m)

    def over_mp(d):
        return remote(vsum, vmp.at[d], v2s.at[d], v2r.at[d], r, mp_at(d))

    for d in range(1, n):
        over_rep(d).start()
    for e in order[early:-1]:
        next_second(e).start()
    acc = vown[...]
    for d in range(1, n):
        over_rep(d).wait_recv()
        acc = acc + vrep[d]
    vsum[...] = acc
    for d in range(1, q):
        over_mp(d).start()
    own_n.wait()

    def pass_on(es):
        for e in es:
            if e:
                next_second(e).wait_recv()
            for d in range(1, lines):
                next_third(e, d).start()

    def share_chip(es):
        for e in es:
            for d in range(1, lines):
                next_third(e, d).wait_recv()
            next_fourth(e).start()

    def ready(es):
        for e in es:
            next_fourth(e).wait_recv()

    pass_on(order[:1])
    for d in range(1, q):
        over_mp(d).wait_recv()
        acc = acc + vmp[d]
    pass_on(order[1:early])

    entry = {}
    lane1 = lax.broadcasted_iota(jnp.int32, (1, 128), 1)
    for s in range(n):
        for t in range(s, n):
            entry[s, t] = jnp.sum(jnp.where(lane1 == t, acc[s : s + 1, :], 0.0), axis=1, keepdims=True)
    coef = mix(entry, n)
    w_copy.wait()
    ct = min(64, rows)

    def combine(c):
        cols = slice(c * half, (c + 1) * half)

        def chunk(a, _):
            span = pl.ds(pl.multiple_of(a * ct, ct), ct)
            update = coef[0] * g[0, span, cols]
            for s in range(1, n):
                update = update + coef[s] * g[s, span, cols]
            wnew[span, cols] = (w_ref[span, cols].astype(F32) - learning_rate * update).astype(BF16)
            return 0

        lax.fori_loop(0, rows // ct, chunk, 0)

    def partial(block, c):
        return jnp.dot(nfull[block], wnew[:, c * half : (c + 1) * half], preferred_element_type=F32)

    def send(way, c, t):
        return remote(
            sbuf.at[way, c, t], rbuf.at[way, c, t], rss.at[way, c, t], rsr.at[way, c, t], (right, left)[way], m
        )

    def stage(way, c, t, add):
        shift = (H - t) * (1 - 2 * way)
        value = partial(ring_rep(lax.rem(p + n + shift, n), n), c)
        if add:
            send(way, c, t - 1).wait_recv()
            value = value + rbuf[way, c, t - 1].astype(F32)
        sbuf[way, c, t] = value.astype(BF16)
        send(way, c, t).start()

    combine(0)
    share_chip(order[:1])
    pass_on(order[early : early + 2])
    combine(1)
    w_back = pltpu.make_async_copy(wnew, w_out, loc.at[0])
    w_back.start()
    ready(order[:1])
    stage(0, 0, 0, False)
    stage(1, 1, 0, False)
    pass_on(order[early + 2 :])
    share_chip(order[1:early])
    for t in range(1, H):
        if t + 1 < H:
            share_chip(order[2 * t + 1 : 2 * t + 3])
        else:
            share_chip(order[2 * t + 1 :])
        ready(order[2 * t - 1 : 2 * t + 1])
        for way, c in ((0, 1), (1, 0), (0, 0), (1, 1)):
            stage(way, c, t, t > 1 or way == c)
    ready(order[-1:])
    scale = n_hbm.shape[1] ** (-0.5)
    for c in range(2):
        value = partial(r, c)
        for way in (1 - c, c):
            send(way, c, H - 1).wait_recv()
            value = value + rbuf[way, c, H - 1].astype(F32)
        out[:, c * half : (c + 1) * half] = (value * scale).astype(BF16)

    back = pltpu.make_async_copy(out, q_out, loc.at[1])
    back.start()
    for d in range(1, q):
        first(d).wait_send()
        over_mp(d).wait_send()
    for d in range(1, lines):
        third(d).wait_send()
        for e in range(n):
            next_third(e, d).wait_send()
    fourth().wait_send()
    for e in range(n):
        next_fourth(e).wait_send()
    for d in range(1, n):
        second_tokens(d).wait_send()
        next_second(d).wait_send()
        over_rep(d).wait_send()

    def drain(j, _):
        for way in range(2):
            for c in range(2):
                gather(way, c, j).wait_send()
                send(way, c, j + 1).wait_send()
        return 0

    lax.fori_loop(0, H - 1, drain, 0)
    for way in range(2):
        gather(way, way, H - 1).wait_send()
        send(way, way, 0).wait_send()
    w_back.wait()
    back.wait()


def local(n, q, weight, tokens, cotangent, next_tokens):
    rows, width = weight.shape
    per = cotangent.shape[0]
    H = n // 2
    dma = pltpu.SemaphoreType.DMA
    vm = pltpu.VMEM
    return pl.pallas_call(
        functools.partial(kernel, n, q),
        out_shape=(
            pltpu.VMEM((rows, width), BF16),
            pltpu.VMEM((per, width), BF16),
        ),
        in_specs=[
            pl.BlockSpec(memory_space=pl.ANY) for _ in range(4)
        ],
        out_specs=(pl.BlockSpec(memory_space=pltpu.VMEM), pl.BlockSpec(memory_space=pltpu.VMEM)),
        scratch_shapes=[
            vm((rows, width), BF16),
            vm((per, width), BF16),
            vm((rows, width), BF16),
            vm((q, per // q, width), BF16),
            vm((n, per, rows), BF16),
            vm((n, per, width), BF16),
            vm((n, per, rows), BF16),
            vm((n, rows, width), F32),
            vm((n * n, 8, 128), F32),
            vm((n, 128), F32),
            vm((n, n, 128), F32),
            vm((n, 128), F32),
            vm((q, n, 128), F32),
            vm((2, 2, H, per, width // 2), BF16),
            vm((2, 2, H, per, width // 2), BF16),
            dma((4,)),
            dma((q,)), dma((q,)), dma((n,)), dma((n,)), dma((q,)), dma((q,)),
            dma((n,)), dma((n,)), dma((q // 2, n)), dma((q // 2, n)), dma((n,)), dma((n,)),
            dma((2, 2, H)), dma((2, 2, H)),
            dma((n,)), dma((n,)), dma((q,)), dma((q,)),
            dma((2, 2, H)), dma((2, 2, H)),
        ],
        compiler_params=pltpu.CompilerParams(
            collective_id=0, has_side_effects=True, vmem_limit_bytes=62 << 20
        ),
    )(weight, tokens, cotangent, next_tokens)


def solution(mesh):
    n, q = mesh.shape["rep"], mesh.shape["mp"]
    in_specs = (P("rep", "mp"), P("rep", "mp"), P("rep", "mp"), P("rep", None))
    out_specs = (P("rep", "mp"), P("rep", "mp"))
    return jax.shard_map(
        functools.partial(local, n, q), mesh=mesh, in_specs=in_specs, out_specs=out_specs, check_vma=False
    )
```
